256 devices in a mesh: pos: 16 (over x, y_hi, core), filt: 8 (over z), layer: 2 (over y_lo).
Axes of the slice: x: 4, y: 4 (y_hi: 2, y_lo: 2; y = y_hi * 2 + y_lo), z: 8, core: 2. Of those that a mesh axis runs over, the one named last changes fastest.
Arguments:
- activations: float32 [512, 1024, 128], P('pos', ('layer', 'filt')), may hold values from -6 to 6
- filters: float32 [9, 1024, 1024], P(None, ('layer', 'pos'), 'filt'), may hold values from -0.0625 to 0.0625
Outputs:
- rectified: float32 [512, 1024, 128], P('pos', ('filt', 'layer'))
The draws below stay inside these ranges and needn't reach their ends.
All inputs are finite; a program needn't handle non-finite values.
Results may differ from the reference program's by a relative error of at most 0.0001.
Values sent between devices are 32-bit elements; how exact they have to be, the bound alone decides.
A program may use at most 128 MiB of HBM per device.

```python
import jax
import jax.numpy as jnp
from jax import lax

CIN = 1024
COUT = 1024
COLS = 128
HEIGHT = 512


def level_of(key, extent, shards, smallest, high):
    factor_of = 1.0
    for position, shards_of in shards:
        heights = jax.random.uniform(jax.random.fold_in(jax.random.fold_in(key, 6), position), (shards_of,), jnp.float32, smallest / len(shards), high / len(shards))
        factor_of = factor_of * jnp.repeat(jnp.exp(heights), extent[position] // shards_of).reshape((-1,) + (1,) * (len(extent) - 1 - position))
    return factor_of


def noise(stream_key, shape, width, most, cuts=(), kind=jnp.bfloat16):
    level = level_of(stream_key, shape, cuts, -0.22, 0.18) if cuts else 1.0
    array = jax.random.normal(stream_key, shape, jnp.float32) * width * level
    return jnp.minimum(jnp.maximum(array, -most), most).astype(kind)


def setup_inputs(seed: int = 0) -> dict:
    key_of = jax.random.split(jax.random.key(seed), 3)
    return {
        "activations": noise(key_of[0], (HEIGHT, CIN, COLS), 1.0, 6.0, ((0, 16), (1, 16)), jnp.float32),
        "filters": noise(key_of[1], (9, CIN, COUT), (9 * CIN) ** -0.5, 0.0625, ((1, 32), (2, 8)), jnp.float32),
    }


def reference(activations, filters):
    height = activations.shape[0]
    across = activations.shape[2]
    padded = jnp.pad(activations, ((1, 1), (0, 0), (1, 1)))
    summed = jnp.zeros((height, filters.shape[2], across), jnp.float32)
    for tap_index in range(9):
        row_shift, col_shift = divmod(tap_index, 3)
        window = padded[row_shift:row_shift + height, :, col_shift:col_shift + across]
        summed = summed + jnp.einsum('ric,io->roc', window, filters[tap_index], precision=lax.Precision.HIGHEST)
    return jnp.maximum(summed, 0.0)
```

```python
import jax
import jax.numpy as jnp
from jax import lax
from jax.experimental import pallas as pl
from jax.experimental.pallas import tpu as pltpu
from jax.sharding import PartitionSpec as P

MESH = pl.DeviceIdType.MESH
F32 = jnp.float32
BF16 = jnp.bfloat16
RING = 8
AHEAD = 4


def halves(value):
    high = value.astype(BF16)
    return high, (value - high.astype(F32)).astype(BF16)


def kernel(act, filt, out, ext, taps, xh, xl, wh, wl, part, other,
           loc_sem, halo_send, halo_recv, w_send, w_recv, z_send, z_recv, r_send, r_recv):
    places = lax.axis_size("pos")
    pos, z, layer = lax.axis_index("pos"), lax.axis_index("filt"), lax.axis_index("layer")
    rows, own, cols = act.shape
    depth = filt.shape[1]
    filters = filt.shape[2]
    channels = RING * own
    chunks = (rows + 2) // 2
    chips = places // 2
    core = lax.rem(pos, 2)
    chip = pos // 2
    mate = pos + 1 - 2 * core
    up, down = lax.rem(z + 1, RING), lax.rem(z + RING - 1, RING)
    turn = 1 - 2 * core
    kept = filters // 2

    def remote(src, dst, send, recv, **where):
        return pltpu.make_async_remote_copy(
            src_ref=src, dst_ref=dst, send_sem=send, recv_sem=recv,
            device_id=where, device_id_type=MESH,
        )

    def panel(source, i):
        return ext.at[source, pl.ds(2 * i, 2)]

    def hop(i, slot, source, target):
        block = panel(source, i)
        return remote(block, block, z_send.at[i, slot], z_recv.at[i, slot], filt=target)

    def weights(place):
        return taps.at[:, pl.ds(pl.multiple_of(place * depth, depth), depth)]

    local = pltpu.make_async_copy(act, ext.at[z, pl.ds(1, rows)], loc_sem.at[0])
    local.start()
    local_w = pltpu.make_async_copy(filt, weights(pos), loc_sem.at[1])
    local_w.start()

    @pl.when(pos == 0)
    def _():
        ext[z, 0] = jnp.zeros((own, cols), F32)

    @pl.when(pos == places - 1)
    def _():
        ext[z, rows + 1] = jnp.zeros((own, cols), F32)

    barrier = pltpu.get_barrier_semaphore()
    pl.semaphore_signal(barrier, inc=1, device_id={"filt": up}, device_id_type=MESH)
    pl.semaphore_signal(barrier, inc=1, device_id={"filt": down}, device_id_type=MESH)
    pl.semaphore_signal(barrier, inc=1, device_id={"layer": 1 - layer}, device_id_type=MESH)
    for d in range(1, places):
        pl.semaphore_signal(barrier, inc=1, device_id={"pos": lax.rem(pos + d, places)}, device_id_type=MESH)
    pl.semaphore_wait(barrier, places + 2)

    below = remote(act.at[rows - 1], ext.at[z, 0], halo_send.at[0], halo_recv.at[0], pos=lax.rem(pos + 1, places))
    above = remote(act.at[0], ext.at[z, rows + 1], halo_send.at[1], halo_recv.at[1], pos=lax.rem(pos + places - 1, places))

    @pl.when(pos < places - 1)
    def _():
        below.start()

    @pl.when(pos > 0)
    def _():
        above.start()

    def first(i):
        hop(i, 0, z, up).start()
        hop(i, 1, z, down).start()

    local.wait()
    for i in range(1, AHEAD):
        first(i)
    mine = remote(filt, weights(pos), w_send.at[0], w_recv.at[0], pos=mate)
    mine.start()

    def straight(d):
        target = lax.rem(chip + d, chips) * 2 + core
        return remote(filt, weights(pos), w_send.at[d], w_recv.at[d], pos=target)

    def relay(d):
        block = weights(lax.rem(chip + chips - d, chips) * 2 + core)
        return remote(block, block, w_send.at[chips + d], w_recv.at[chips + d], pos=mate)

    def arrived(d):
        block = weights(lax.rem(chip + chips - d, chips) * 2 + core)
        return remote(block, block, w_send.at[d], w_recv.at[d], pos=mate)

    def relayed(d):
        block = weights(lax.rem(chip + chips - d, chips) * 2 + 1 - core)
        return remote(block, block, w_send.at[chips + d], w_recv.at[chips + d], pos=mate)

    for d in range(1, chips):
        straight(d).start()

    @pl.when(pos > 0)
    def _():
        below.wait_recv()

    first(0)

    def split_rows(r):
        high, low = halves(ext[:, r].reshape(channels, cols))
        xh[r] = high
        xl[r] = low

    def split_taps(t, carry):
        a, b = t // 3, lax.rem(t, 3)
        high, low = halves(taps[t].T)
        at = pl.ds(pl.multiple_of(b * filters, filters), filters)
        wh[a, at] = high
        wl[a, at] = low
        return carry

    lanes = lax.broadcasted_iota(jnp.int32, (filters, cols), 1)

    def swap(k):
        theirs = pl.ds(pl.multiple_of((1 - layer) * kept, kept), kept)
        return remote(part.at[k, :, theirs], other.at[k], r_send.at[k], r_recv.at[k], layer=1 - layer)

    def convolve(k):
        total = None
        for a in range(3):
            high = jnp.concatenate([xh[2 * k + a], xh[2 * k + a + 1]], axis=1)
            low = jnp.concatenate([xl[2 * k + a], xl[2 * k + a + 1]], axis=1)
            for left, right in ((wh, high), (wl, high), (wh, low)):
                term = jnp.dot(left[a], right, preferred_element_type=F32)
                total = term if total is None else total + term
        for q in range(2):
            left, middle, right = [
                total[b * filters : (b + 1) * filters, q * cols : (q + 1) * cols] for b in range(3)
            ]
            left = jnp.where(lanes == 0, 0.0, pltpu.roll(left, 1, 1))
            right = jnp.where(lanes == cols - 1, 0.0, pltpu.roll(right, cols - 1, 1))
            part[k, q] = middle + left + right
        swap(k).start()

    def finish(k):
        swap(k).wait_recv()
        ours = pl.ds(pl.multiple_of(layer * kept, kept), kept)
        out[pl.ds(2 * k, 2)] = part[k, :, ours] + other[k]

    def step(t, carry):
        i = t + AHEAD

        @pl.when(i < chunks)
        def _():
            @pl.when((i == chunks - 1) & (pos < places - 1))
            def _():
                above.wait_recv()

            first(i)

        for h in range(1, 4):
            i = t - (h - 1)

            @pl.when((i >= 0) & (i < chunks))
            def _():
                behind, ahead = lax.rem(z + RING - h, RING), lax.rem(z + h, RING)
                hop(i, 2 * h - 2, behind, up).wait_recv()
                if h < 3:
                    hop(i, 2 * h, behind, up).start()
                hop(i, 2 * h - 1, ahead, down).wait_recv()
                if h < 3:
                    hop(i, 2 * h + 1, ahead, down).start()
                else:
                    hop(i, 6, lax.rem(z + RING - 3 * turn, RING), lax.rem(z + RING + turn, RING)).start()

        for early in range(3):
            @pl.when(t == early)
            def _():
                for d in range(1, chips):
                    if (d - 1) * 3 // (chips - 1) == early:
                        arrived(d).wait_recv()
                        relay(d).start()

        @pl.when(t == 3)
        def _():
            local_w.wait()
            remote(filt, weights(mate), w_send.at[0], w_recv.at[0], pos=mate).wait_recv()
            for d in range(1, chips):
                relayed(d).wait_recv()
            lax.fori_loop(0, 9, split_taps, 0)

        @pl.when(t >= 3)
        def _():
            i = t - 3
            hop(i, 6, lax.rem(z + 4, RING), up).wait_recv()
            split_rows(2 * i)
            split_rows(2 * i + 1)

        @pl.when(t >= 5)
        def _():
            finish(t - 5)

        @pl.when(t >= 4)
        def _():
            convolve(t - 4)

        return carry

    lax.fori_loop(0, chunks + 3, step, 0)
    finish(chunks - 2)

    def drain(i, carry):
        for slot in range(7):
            hop(i, slot, z, up).wait_send()
        return carry

    lax.fori_loop(0, chunks, drain, 0)

    def drain_swap(k, carry):
        swap(k).wait_send()
        return carry

    lax.fori_loop(0, chunks - 1, drain_swap, 0)
    mine.wait_send()
    for d in range(1, chips):
        straight(d).wait_send()
        relay(d).wait_send()

    @pl.when(pos < places - 1)
    def _():
        below.wait_send()

    @pl.when(pos > 0)
    def _():
        above.wait_send()


def body(activations, filters):
    rows, own, cols = activations.shape
    places = lax.axis_size("pos")
    depth, count = filters.shape[1], filters.shape[2]
    channels = RING * own
    chunks = (rows + 2) // 2
    dma = pltpu.SemaphoreType.DMA
    summed = pl.pallas_call(
        kernel,
        out_shape=jax.ShapeDtypeStruct((rows, count // 2, cols), F32),
        in_specs=[pl.BlockSpec(memory_space=pl.ANY)] * 2,
        out_specs=pl.BlockSpec(memory_space=pltpu.VMEM),
        scratch_shapes=[
            pltpu.VMEM((RING, rows + 2, own, cols), F32),
            pltpu.VMEM((9, places * depth, count), F32),
            pltpu.VMEM((rows + 2, channels, cols), BF16),
            pltpu.VMEM((rows + 2, channels, cols), BF16),
            pltpu.VMEM((3, 3 * count, channels), BF16),
            pltpu.VMEM((3, 3 * count, channels), BF16),
            pltpu.VMEM((rows // 2, 2, count, cols), F32),
            pltpu.VMEM((rows // 2, 2, count // 2, cols), F32),
            dma((2,)),
            dma((2,)),
            dma((2,)),
            dma((places,)),
            dma((places,)),
            dma((chunks, 7)),
            dma((chunks, 7)),
            dma((rows // 2,)),
            dma((rows // 2,)),
        ],
        compiler_params=pltpu.CompilerParams(
            collective_id=0, has_side_effects=True, vmem_limit_bytes=48 << 20
        ),
    )(activations, filters)
    return jnp.maximum(summed, 0.0)


def solution(mesh):
    in_specs = (P("pos", ("layer", "filt"), None), P(None, ("layer", "pos"), "filt"))
    out_specs = P("pos", ("filt", "layer"), None)
    return jax.shard_map(body, mesh=mesh, in_specs=in_specs, out_specs=out_specs, check_vma=False)
```

```python
import jax
import jax.numpy as jnp
from jax import lax
from jax.experimental import pallas as pl
from jax.experimental.pallas import tpu as pltpu
from jax.sharding import PartitionSpec as P

MESH = pl.DeviceIdType.MESH
F32 = jnp.float32
BF16 = jnp.bfloat16
RING = 8
AHEAD = 2
RUN = 4
READY = 3
RELAYS = ((1, (1, 2, 3)), (2, (4, 5, 6, 7)))
EDGES = 7


def halves(value):
    high = value.astype(BF16)
    return high, (value - high.astype(F32)).astype(BF16)


def kernel(act, filt, out, ext, edge, taps, xh, xl, wh, wl, theirs, ours, other,
           loc_sem, halo_send, halo_recv, w_send, w_recv, z_send, z_recv, r_send, r_recv):
    places = lax.axis_size("pos")
    pos, z, layer = lax.axis_index("pos"), lax.axis_index("filt"), lax.axis_index("layer")
    rows, own, cols = act.shape
    depth = filt.shape[1]
    filters = filt.shape[2]
    channels = RING * own
    chunks = rows // RUN
    pairs = rows // 2
    chips = places // 2
    core = lax.rem(pos, 2)
    chip = pos // 2
    mate = pos + 1 - 2 * core
    up, down = lax.rem(z + 1, RING), lax.rem(z + RING - 1, RING)
    turn = 1 - 2 * core
    kept = filters // 2

    def remote(src, dst, send, recv, **where):
        return pltpu.make_async_remote_copy(
            src_ref=src, dst_ref=dst, send_sem=send, recv_sem=recv,
            device_id=where, device_id_type=MESH,
        )

    def panel(source, i):
        return ext.at[source, pl.ds(RUN * i, RUN)]

    def hop(i, slot, source, target):
        block = panel(source, i)
        return remote(block, block, z_send.at[i, slot], z_recv.at[i, slot], filt=target)

    def weights(place):
        return taps.at[:, pl.ds(pl.multiple_of(place * depth, depth), depth)]

    local = [
        pltpu.make_async_copy(act.at[0], ext.at[z, 0], loc_sem.at[0]),
        pltpu.make_async_copy(act.at[rows - 1], ext.at[z, 1], loc_sem.at[2]),
        pltpu.make_async_copy(act.at[pl.ds(1, rows - 2)], ext.at[z, pl.ds(2, rows - 2)], loc_sem.at[3]),
    ]
    for copy in local:
        copy.start()
    local_w = pltpu.make_async_copy(filt, weights(pos), loc_sem.at[1])
    local_w.start()

    @pl.when(pos == 0)
    def _():
        edge[0] = jnp.zeros((RING, own, cols), F32)

    @pl.when(pos == places - 1)
    def _():
        edge[1] = jnp.zeros((RING, own, cols), F32)

    barrier = pltpu.get_barrier_semaphore()
    pl.semaphore_signal(barrier, inc=1, device_id={"filt": up}, device_id_type=MESH)
    pl.semaphore_signal(barrier, inc=1, device_id={"filt": down}, device_id_type=MESH)
    pl.semaphore_signal(barrier, inc=1, device_id={"layer": 1 - layer}, device_id_type=MESH)
    for d in range(1, places):
        pl.semaphore_signal(barrier, inc=1, device_id={"pos": lax.rem(pos + d, places)}, device_id_type=MESH)
    pl.semaphore_wait(barrier, places + 2)

    below = remote(ext.at[:, 1], edge.at[0], halo_send.at[0], halo_recv.at[0], pos=lax.rem(pos + 1, places))
    above = remote(ext.at[:, 0], edge.at[1], halo_send.at[1], halo_recv.at[1], pos=lax.rem(pos + places - 1, places))

    def first(i):
        hop(i, 0, z, up).start()
        hop(i, 1, z, down).start()

    for copy in local:
        copy.wait()
    for i in range(AHEAD):
        first(i)
    mine = remote(filt, weights(pos), w_send.at[0], w_recv.at[0], pos=mate)
    mine.start()

    def straight(d):
        target = lax.rem(chip + d, chips) * 2 + core
        return remote(filt, weights(pos), w_send.at[d], w_recv.at[d], pos=target)

    def relay(d):
        block = weights(lax.rem(chip + chips - d, chips) * 2 + core)
        return remote(block, block, w_send.at[chips + d], w_recv.at[chips + d], pos=mate)

    def arrived(d):
        block = weights(lax.rem(chip + chips - d, chips) * 2 + core)
        return remote(block, block, w_send.at[d], w_recv.at[d], pos=mate)

    def relayed(d):
        block = weights(lax.rem(chip + chips - d, chips) * 2 + 1 - core)
        return remote(block, block, w_send.at[chips + d], w_recv.at[chips + d], pos=mate)

    for d in range(1, chips):
        straight(d).start()

    def split_rows(r, block):
        high, low = halves(block.reshape(channels, cols))
        xh[r] = high
        xl[r] = low

    def split_taps(t, carry):
        a, b = t // 3, lax.rem(t, 3)
        high, low = halves(taps[t].T)
        at = pl.ds(pl.multiple_of(b * kept, kept), kept)
        for owner in range(2):
            side = 1 - owner + layer * (2 * owner - 1)
            taken = slice(owner * kept, (owner + 1) * kept)
            wh[a, side, at] = high[taken]
            wl[a, side, at] = low[taken]
        return carry

    lanes = lax.broadcasted_iota(jnp.int32, (kept, cols), 1)

    def swap(k):
        return remote(theirs.at[k], other.at[k], r_send.at[k], r_recv.at[k], layer=1 - layer)

    def convolve(k, sides):
        first_side, count = sides[0], len(sides)
        height = count * 3 * kept
        total = None
        for a in range(3):
            high = jnp.concatenate([xh[2 * k + a], xh[2 * k + a + 1]], axis=1)
            low = jnp.concatenate([xl[2 * k + a], xl[2 * k + a + 1]], axis=1)
            for left, right in ((wh, high), (wl, high), (wh, low)):
                left = left[a, first_side : first_side + count].reshape(height, channels)
                term = jnp.dot(left, right, preferred_element_type=F32)
                total = term if total is None else total + term
        for n, side in enumerate(sides):
            for q in range(2):
                left, middle, right = [
                    total[(3 * n + b) * kept : (3 * n + b + 1) * kept, q * cols : (q + 1) * cols] for b in range(3)
                ]
                left = jnp.where(lanes == 0, 0.0, pltpu.roll(left, 1, 1))
                right = jnp.where(lanes == cols - 1, 0.0, pltpu.roll(right, cols - 1, 1))
                (theirs, ours)[side][k, q] = middle + left + right

    def whole(k, carry):
        convolve(k, (0, 1))
        swap(k).start()
        return carry

    def finish(k, carry):
        swap(k).wait_recv()
        out[pl.ds(2 * k, 2)] = ours[k] + other[k]
        return carry

    def settle(i):
        hop(i, 6, lax.rem(z + 4, RING), up).wait_recv()

    def split_chunk(i):
        for n in range(RUN):
            split_rows(RUN * i + n, ext[:, RUN * i + n])

    def step(t, carry):
        i = t + AHEAD

        @pl.when(i < chunks)
        def _():
            first(i)

        def through(h):
            i = t - (h - 1)

            @pl.when((i >= 0) & (i < chunks))
            def _():
                behind, ahead = lax.rem(z + RING - h, RING), lax.rem(z + h, RING)
                hop(i, 2 * h - 2, behind, up).wait_recv()
                if h < 3:
                    hop(i, 2 * h, behind, up).start()
                hop(i, 2 * h - 1, ahead, down).wait_recv()
                if h < 3:
                    hop(i, 2 * h + 1, ahead, down).start()
                else:
                    hop(i, 6, lax.rem(z + RING - 3 * turn, RING), lax.rem(z + RING + turn, RING)).start()

        fresh = t >= 5
        k = RUN // 2 * (t - 4) - 1

        through(1)

        @pl.when(fresh)
        def _():
            whole(k, 0)

        through(2)

        @pl.when(fresh)
        def _():
            whole(k + 1, 0)

        through(3)

        for early, group in RELAYS:
            @pl.when(t == early)
            def _():
                for d in group:
                    arrived(d).wait_recv()
                    relay(d).start()

        @pl.when(t == READY)
        def _():
            local_w.wait()
            remote(filt, weights(mate), w_send.at[0], w_recv.at[0], pos=mate).wait_recv()
            for d in range(1, chips):
                relayed(d).wait_recv()
            lax.fori_loop(0, 9, split_taps, 0)

        @pl.when(t == EDGES)
        def _():
            @pl.when(pos > 0)
            def _():
                below.wait_recv()

            @pl.when(pos < places - 1)
            def _():
                above.wait_recv()

            split_rows(0, edge[0])
            split_rows(rows + 1, edge[1])
            whole(0, 0)

        @pl.when(t >= 6)
        def _():
            finish(k - 2, 0)
            finish(k - 1, 0)

        @pl.when(t == 3)
        def _():
            settle(0)

            @pl.when(pos < places - 1)
            def _():
                below.start()

            @pl.when(pos > 0)
            def _():
                above.start()

            split_rows(1, ext[:, 0])
            split_rows(rows, ext[:, 1])
            split_rows(2, ext[:, 2])
            split_rows(3, ext[:, 3])

        @pl.when(t > 3)
        def _():
            settle(t - 3)
            split_chunk(t - 3)

        return carry

    lax.fori_loop(0, chunks + 3, step, 0)
    late = pairs - 3
    lax.fori_loop(late, pairs, lambda k, carry: (convolve(k, (0,)), swap(k).start(), carry)[2], 0)
    finish(0, 0)
    finish(late - 2, 0)
    finish(late - 1, 0)
    lax.fori_loop(late, pairs, lambda k, carry: (convolve(k, (1,)), carry)[1], 0)
    lax.fori_loop(late, pairs, finish, 0)

    def drain(i, carry):
        for slot in range(7):
            hop(i, slot, z, up).wait_send()
        return carry

    lax.fori_loop(0, chunks, drain, 0)

    def drain_swap(k, carry):
        swap(k).wait_send()
        return carry

    lax.fori_loop(0, pairs, drain_swap, 0)
    mine.wait_send()
    for d in range(1, chips):
        straight(d).wait_send()
        relay(d).wait_send()

    @pl.when(pos < places - 1)
    def _():
        below.wait_send()

    @pl.when(pos > 0)
    def _():
        above.wait_send()


def body(activations, filters):
    rows, own, cols = activations.shape
    places = lax.axis_size("pos")
    depth, count = filters.shape[1], filters.shape[2]
    channels = RING * own
    chunks = rows // RUN
    dma = pltpu.SemaphoreType.DMA
    summed = pl.pallas_call(
        kernel,
        out_shape=jax.ShapeDtypeStruct((rows, count // 2, cols), F32),
        in_specs=[pl.BlockSpec(memory_space=pl.ANY)] * 2,
        out_specs=pl.BlockSpec(memory_space=pltpu.VMEM),
        scratch_shapes=[
            pltpu.VMEM((RING, rows, own, cols), F32),
            pltpu.VMEM((2, RING, own, cols), F32),
            pltpu.VMEM((9, places * depth, count), F32),
            pltpu.VMEM((rows + 2, channels, cols), BF16),
            pltpu.VMEM((rows + 2, channels, cols), BF16),
            pltpu.VMEM((3, 2, 3 * count // 2, channels), BF16),
            pltpu.VMEM((3, 2, 3 * count // 2, channels), BF16),
            pltpu.VMEM((rows // 2, 2, count // 2, cols), F32),
            pltpu.VMEM((rows // 2, 2, count // 2, cols), F32),
            pltpu.VMEM((rows // 2, 2, count // 2, cols), F32),
            dma((4,)),
            dma((2,)),
            dma((2,)),
            dma((places,)),
            dma((places,)),
            dma((chunks, 7)),
            dma((chunks, 7)),
            dma((rows // 2,)),
            dma((rows // 2,)),
        ],
        compiler_params=pltpu.CompilerParams(
            collective_id=0, has_side_effects=True, vmem_limit_bytes=67043328
        ),
    )(activations, filters)
    return jnp.maximum(summed, 0.0)


def solution(mesh):
    in_specs = (P("pos", ("layer", "filt"), None), P(None, ("layer", "pos"), "filt"))
    out_specs = P("pos", ("filt", "layer"), None)
    return jax.shard_map(body, mesh=mesh, in_specs=in_specs, out_specs=out_specs, check_vma=False)
```

```python
import jax
import jax.numpy as jnp
from jax import lax
from jax.experimental import pallas as pl
from jax.experimental.pallas import tpu as pltpu
from jax.sharding import PartitionSpec as P

MESH = pl.DeviceIdType.MESH
F32 = jnp.float32
BF16 = jnp.bfloat16
RING = 8
AHEAD = 2
RUN = 4
READY = 3
RELAYS = ((0, (1, 2, 3)), (1, (4, 5, 6)), (2, (7,)))
SHARDS = {1: (0, 1), 2: (-1, 0), 3: (1, 0), 4: (-1, 1), 5: (1, 1), 6: (-2, 0), 7: (2, 1)}
EDGES = 7


def halves(value):
    high = value.astype(BF16)
    return high, (value - high.astype(F32)).astype(BF16)


def kernel(act, filt, out, ext, edge, taps, xh, xl, wh, wl, theirs, ours, other,
           loc_sem, halo_send, halo_recv, w_send, w_recv, z_send, z_recv, r_send, r_recv):
    places = lax.axis_size("pos")
    pos, z, layer = lax.axis_index("pos"), lax.axis_index("filt"), lax.axis_index("layer")
    rows, own, cols = act.shape
    depth = filt.shape[1]
    filters = filt.shape[2]
    channels = RING * own
    chunks = rows // RUN
    pairs = rows // 2
    across = places // 4
    core = lax.rem(pos, 2)
    half = lax.rem(pos // 2, 2)
    facing = pos + 2 - 4 * half
    after, before = lax.rem(pos + 4, places), lax.rem(pos + places - 4, places)
    mate = pos + 1 - 2 * core
    up, down = lax.rem(z + 1, RING), lax.rem(z + RING - 1, RING)
    turn = 1 - 2 * core
    kept = filters // 2

    def remote(src, dst, send, recv, **where):
        return pltpu.make_async_remote_copy(
            src_ref=src, dst_ref=dst, send_sem=send, recv_sem=recv,
            device_id=where, device_id_type=MESH,
        )

    def panel(source, i):
        return ext.at[source, pl.ds(RUN * i, RUN)]

    def hop(i, slot, source, target):
        block = panel(source, i)
        return remote(block, block, z_send.at[i, slot], z_recv.at[i, slot], filt=target)

    def weights(place):
        return taps.at[:, pl.ds(pl.multiple_of(place * depth, depth), depth)]

    local = [
        pltpu.make_async_copy(act.at[0], ext.at[z, 0], loc_sem.at[0]),
        pltpu.make_async_copy(act.at[rows - 1], ext.at[z, 1], loc_sem.at[2]),
        pltpu.make_async_copy(act.at[pl.ds(1, rows - 2)], ext.at[z, pl.ds(2, rows - 2)], loc_sem.at[3]),
    ]
    for copy in local:
        copy.start()
    local_w = pltpu.make_async_copy(filt, weights(pos), loc_sem.at[1])
    local_w.start()

    @pl.when(pos == 0)
    def _():
        edge[0] = jnp.zeros((RING, own, cols), F32)

    @pl.when(pos == places - 1)
    def _():
        edge[1] = jnp.zeros((RING, own, cols), F32)

    barrier = pltpu.get_barrier_semaphore()
    pl.semaphore_signal(barrier, inc=1, device_id={"filt": up}, device_id_type=MESH)
    pl.semaphore_signal(barrier, inc=1, device_id={"filt": down}, device_id_type=MESH)
    pl.semaphore_signal(barrier, inc=1, device_id={"layer": 1 - layer}, device_id_type=MESH)
    near = (lax.rem(pos + 1, places), lax.rem(pos + places - 1, places), after, before, facing)
    for place in near:
        pl.semaphore_signal(barrier, inc=1, device_id={"pos": place}, device_id_type=MESH)
    pl.semaphore_wait(barrier, len(near) + 3)

    below = remote(ext.at[:, 1], edge.at[0], halo_send.at[0], halo_recv.at[0], pos=lax.rem(pos + 1, places))
    above = remote(ext.at[:, 0], edge.at[1], halo_send.at[1], halo_recv.at[1], pos=lax.rem(pos + places - 1, places))

    def first(i):
        hop(i, 0, z, up).start()
        hop(i, 1, z, down).start()

    for copy in local:
        copy.wait()
    for i in range(AHEAD):
        first(i)
    def shard(n, side):
        dx, flip = SHARDS[n]
        row = lax.rem(pos // 4 + across + dx, across)
        return weights(4 * row + 2 * (1 - half if flip else half) + side)

    own_sends = [
        remote(filt, weights(pos), w_send.at[0], w_recv.at[0], pos=mate),
        remote(filt, weights(pos), w_send.at[1], w_recv.at[1], pos=facing),
        remote(filt, weights(pos), w_send.at[2], w_recv.at[2], pos=after),
        remote(filt, weights(pos), w_send.at[3], w_recv.at[3], pos=before),
    ]
    onward = ((1, 4, after), (1, 5, before), (2, 6, after), (5, 7, before))

    def relays(n):
        block = shard(n, core)
        sends = [remote(block, block, w_send.at[3 + n], w_recv.at[8 + n], pos=mate)]
        for source, arrival, target in onward:
            if source == n:
                sends.append(remote(block, block, w_send.at[7 + arrival], w_recv.at[arrival], pos=target))
        return sends

    def arrived(n):
        block = shard(n, core)
        return remote(block, block, w_send.at[0], w_recv.at[n], pos=mate)

    def relayed(n):
        block = shard(n, 1 - core)
        return remote(block, block, w_send.at[0], w_recv.at[8 + n], pos=mate)

    for send in own_sends:
        send.start()

    def split_rows(r, block):
        high, low = halves(block.reshape(channels, cols))
        xh[r] = high
        xl[r] = low

    def split_taps(t, carry):
        a, b = t // 3, lax.rem(t, 3)
        high, low = halves(taps[t].T)
        at = pl.ds(pl.multiple_of(b * kept, kept), kept)
        for owner in range(2):
            side = 1 - owner + layer * (2 * owner - 1)
            taken = slice(owner * kept, (owner + 1) * kept)
            wh[a, side, at] = high[taken]
            wl[a, side, at] = low[taken]
        return carry

    lanes = lax.broadcasted_iota(jnp.int32, (kept, cols), 1)

    def swap(k):
        return remote(theirs.at[k], other.at[k], r_send.at[k], r_recv.at[k], layer=1 - layer)

    def convolve(k, sides):
        first_side, count = sides[0], len(sides)
        height = count * 3 * kept
        total = None
        for a in range(3):
            high = jnp.concatenate([xh[2 * k + a], xh[2 * k + a + 1]], axis=1)
            low = jnp.concatenate([xl[2 * k + a], xl[2 * k + a + 1]], axis=1)
            for left, right in ((wh, high), (wl, high), (wh, low)):
                left = left[a, first_side : first_side + count].reshape(height, channels)
                term = jnp.dot(left, right, preferred_element_type=F32)
                total = term if total is None else total + term
        for n, side in enumerate(sides):
            for q in range(2):
                left, middle, right = [
                    total[(3 * n + b) * kept : (3 * n + b + 1) * kept, q * cols : (q + 1) * cols] for b in range(3)
                ]
                left = jnp.where(lanes == 0, 0.0, pltpu.roll(left, 1, 1))
                right = jnp.where(lanes == cols - 1, 0.0, pltpu.roll(right, cols - 1, 1))
                (theirs, ours)[side][k, q] = middle + left + right

    def whole(k, carry):
        convolve(k, (0, 1))
        swap(k).start()
        return carry

    def finish(k, carry):
        swap(k).wait_recv()
        out[pl.ds(2 * k, 2)] = ours[k] + other[k]
        return carry

    def settle(i):
        hop(i, 6, lax.rem(z + 4, RING), up).wait_recv()

    def split_chunk(i):
        for n in range(RUN):
            split_rows(RUN * i + n, ext[:, RUN * i + n])

    def step(t, carry):
        i = t + AHEAD

        @pl.when(i < chunks)
        def _():
            first(i)

        def through(h):
            i = t - (h - 1)

            @pl.when((i >= 0) & (i < chunks))
            def _():
                behind, ahead = lax.rem(z + RING - h, RING), lax.rem(z + h, RING)
                hop(i, 2 * h - 2, behind, up).wait_recv()
                if h < 3:
                    hop(i, 2 * h, behind, up).start()
                hop(i, 2 * h - 1, ahead, down).wait_recv()
                if h < 3:
                    hop(i, 2 * h + 1, ahead, down).start()
                else:
                    hop(i, 6, lax.rem(z + RING - 3 * turn, RING), lax.rem(z + RING + turn, RING)).start()

        fresh = t >= 5
        k = RUN // 2 * (t - 4) - 1

        through(1)

        @pl.when(fresh)
        def _():
            whole(k, 0)

        through(2)

        @pl.when(fresh)
        def _():
            whole(k + 1, 0)

        through(3)

        for early, group in RELAYS:
            @pl.when(t == early)
            def _():
                for d in group:
                    arrived(d).wait_recv()
                    for send in relays(d):
                        send.start()

        @pl.when(t == READY)
        def _():
            local_w.wait()
            remote(filt, weights(mate), w_send.at[0], w_recv.at[0], pos=mate).wait_recv()
            for d in SHARDS:
                relayed(d).wait_recv()
            lax.fori_loop(0, 9, split_taps, 0)

        @pl.when(t == EDGES)
        def _():
            @pl.when(pos > 0)
            def _():
                below.wait_recv()

            @pl.when(pos < places - 1)
            def _():
                above.wait_recv()

            split_rows(0, edge[0])
            split_rows(rows + 1, edge[1])
            whole(0, 0)

        @pl.when(t >= 6)
        def _():
            finish(k - 2, 0)
            finish(k - 1, 0)

        @pl.when(t == 3)
        def _():
            settle(0)

            @pl.when(pos < places - 1)
            def _():
                below.start()

            @pl.when(pos > 0)
            def _():
                above.start()

            split_rows(1, ext[:, 0])
            split_rows(rows, ext[:, 1])
            split_rows(2, ext[:, 2])
            split_rows(3, ext[:, 3])

        @pl.when(t > 3)
        def _():
            settle(t - 3)
            split_chunk(t - 3)

        return carry

    lax.fori_loop(0, chunks + 3, step, 0)
    late = pairs - 3
    lax.fori_loop(late, pairs, lambda k, carry: (convolve(k, (0,)), swap(k).start(), carry)[2], 0)
    finish(0, 0)
    finish(late - 2, 0)
    finish(late - 1, 0)
    lax.fori_loop(late, pairs, lambda k, carry: (convolve(k, (1,)), carry)[1], 0)
    lax.fori_loop(late, pairs, finish, 0)

    def drain(i, carry):
        for slot in range(7):
            hop(i, slot, z, up).wait_send()
        return carry

    lax.fori_loop(0, chunks, drain, 0)

    def drain_swap(k, carry):
        swap(k).wait_send()
        return carry

    lax.fori_loop(0, pairs, drain_swap, 0)
    for send in own_sends:
        send.wait_send()
    for d in SHARDS:
        for send in relays(d):
            send.wait_send()

    @pl.when(pos < places - 1)
    def _():
        below.wait_send()

    @pl.when(pos > 0)
    def _():
        above.wait_send()


def body(activations, filters):
    rows, own, cols = activations.shape
    places = lax.axis_size("pos")
    depth, count = filters.shape[1], filters.shape[2]
    channels = RING * own
    chunks = rows // RUN
    dma = pltpu.SemaphoreType.DMA
    summed = pl.pallas_call(
        kernel,
        out_shape=jax.ShapeDtypeStruct((rows, count // 2, cols), F32),
        in_specs=[pl.BlockSpec(memory_space=pltpu.HBM)] * 2,
        out_specs=pl.BlockSpec(memory_space=pltpu.VMEM),
        scratch_shapes=[
            pltpu.VMEM((RING, rows, own, cols), F32),
            pltpu.VMEM((2, RING, own, cols), F32),
            pltpu.VMEM((9, places * depth, count), F32),
            pltpu.VMEM((rows + 2, channels, cols), BF16),
            pltpu.VMEM((rows + 2, channels, cols), BF16),
            pltpu.VMEM((3, 2, 3 * count // 2, channels), BF16),
            pltpu.VMEM((3, 2, 3 * count // 2, channels), BF16),
            pltpu.VMEM((rows // 2, 2, count // 2, cols), F32),
            pltpu.VMEM((rows // 2, 2, count // 2, cols), F32),
            pltpu.VMEM((rows // 2, 2, count // 2, cols), F32),
            dma((4,)),
            dma((2,)),
            dma((2,)),
            dma((places,)),
            dma((places,)),
            dma((chunks, 7)),
            dma((chunks, 7)),
            dma((rows // 2,)),
            dma((rows // 2,)),
        ],
        compiler_params=pltpu.CompilerParams(
            collective_id=0, has_side_effects=True, vmem_limit_bytes=34 << 20
        ),
    )(pltpu.with_memory_space_constraint(activations, pltpu.HBM), pltpu.with_memory_space_constraint(filters, pltpu.HBM))
    return jnp.maximum(summed, 0.0)


def solution(mesh):
    in_specs = (P("pos", ("layer", "filt"), None), P(None, ("layer", "pos"), "filt"))
    out_specs = P("pos", ("filt", "layer"), None)
    return jax.shard_map(body, mesh=mesh, in_specs=in_specs, out_specs=out_specs, check_vma=False)
```

```python
import jax
import jax.numpy as jnp
from jax import lax
from jax.experimental import pallas as pl
from jax.experimental.pallas import tpu as pltpu
from jax.sharding import PartitionSpec as P

MESH = pl.DeviceIdType.MESH
F32 = jnp.float32
BF16 = jnp.bfloat16
RING = 8
AHEAD = 2
RUN = 4
READY = 3
RELAYS = ((0, (1, 2, 3)), (1, (4, 5, 6)), (2, (7,)))
SHARDS = {1: (0, 1), 2: (-1, 0), 3: (1, 0), 4: (-1, 1), 5: (1, 1), 6: (-2, 0), 7: (2, 1)}
EDGES = 7


def halves(value):
    high = value.astype(BF16)
    return high, (value - high.astype(F32)).astype(BF16)


def kernel(act, filt, out, ext, edge, taps, xh, xl, wh, wl, theirs, ours, other,
           loc_sem, halo_send, halo_recv, w_send, w_recv, z_send, z_recv, r_send, r_recv):
    places = lax.axis_size("pos")
    pos, z, layer = lax.axis_index("pos"), lax.axis_index("filt"), lax.axis_index("layer")
    rows, own, cols = act.shape
    depth = filt.shape[1]
    filters = filt.shape[2]
    channels = RING * own
    chunks = rows // RUN
    pairs = rows // 2
    across = places // 4
    core = lax.rem(pos, 2)
    half = lax.rem(pos // 2, 2)
    facing = pos + 2 - 4 * half
    after, before = lax.rem(pos + 4, places), lax.rem(pos + places - 4, places)
    mate = pos + 1 - 2 * core
    up, down = lax.rem(z + 1, RING), lax.rem(z + RING - 1, RING)
    turn = 1 - 2 * core
    kept = filters // 2

    def remote(src, dst, send, recv, **where):
        return pltpu.make_async_remote_copy(
            src_ref=src, dst_ref=dst, send_sem=send, recv_sem=recv,
            device_id=where, device_id_type=MESH,
        )

    def panel(source, i):
        return ext.at[source, pl.ds(RUN * i, RUN)]

    def hop(i, slot, source, target):
        block = panel(source, i)
        return remote(block, block, z_send.at[i, slot], z_recv.at[i, slot], filt=target)

    def weights(place):
        return taps.at[:, pl.ds(pl.multiple_of(place * depth, depth), depth)]

    local = [
        pltpu.make_async_copy(act.at[0], ext.at[z, 0], loc_sem.at[0]),
        pltpu.make_async_copy(act.at[rows - 1], ext.at[z, 1], loc_sem.at[2]),
        pltpu.make_async_copy(act.at[pl.ds(1, rows - 2)], ext.at[z, pl.ds(2, rows - 2)], loc_sem.at[3]),
    ]
    for copy in local:
        copy.start()
    local_w = pltpu.make_async_copy(filt, weights(pos), loc_sem.at[1])
    local_w.start()

    @pl.when(pos == 0)
    def _():
        edge[0] = jnp.zeros((RING, own, cols), F32)

    @pl.when(pos == places - 1)
    def _():
        edge[1] = jnp.zeros((RING, own, cols), F32)

    barrier = pltpu.get_barrier_semaphore()
    pl.semaphore_signal(barrier, inc=1, device_id={"filt": up}, device_id_type=MESH)
    pl.semaphore_signal(barrier, inc=1, device_id={"filt": down}, device_id_type=MESH)
    pl.semaphore_signal(barrier, inc=1, device_id={"layer": 1 - layer}, device_id_type=MESH)
    near = (lax.rem(pos + 1, places), lax.rem(pos + places - 1, places), after, before, facing)
    for place in near:
        pl.semaphore_signal(barrier, inc=1, device_id={"pos": place}, device_id_type=MESH)
    pl.semaphore_wait(barrier, len(near) + 3)

    below = remote(ext.at[:, 1], edge.at[0], halo_send.at[0], halo_recv.at[0], pos=lax.rem(pos + 1, places))
    above = remote(ext.at[:, 0], edge.at[1], halo_send.at[1], halo_recv.at[1], pos=lax.rem(pos + places - 1, places))

    def part(n, source, target):
        block = ext.at[source, pl.ds(RUN * (chunks - 1) + 2 * n, 2)]
        at = chunks - 1 + n
        return remote(block, block, z_send.at[at, 6], z_recv.at[at, 6], filt=target)

    def first(i):
        hop(i, 0, z, up).start()
        hop(i, 1, z, down).start()

    for copy in local:
        copy.wait()
    for i in range(AHEAD):
        first(i)
    def shard(n, side):
        dx, flip = SHARDS[n]
        row = lax.rem(pos // 4 + across + dx, across)
        return weights(4 * row + 2 * (1 - half if flip else half) + side)

    own_sends = [
        remote(filt, weights(pos), w_send.at[0], w_recv.at[0], pos=mate),
        remote(filt, weights(pos), w_send.at[1], w_recv.at[1], pos=facing),
        remote(filt, weights(pos), w_send.at[2], w_recv.at[2], pos=after),
        remote(filt, weights(pos), w_send.at[3], w_recv.at[3], pos=before),
    ]
    onward = ((1, 4, after), (1, 5, before), (2, 6, after), (5, 7, before))

    def relays(n):
        block = shard(n, core)
        sends = [remote(block, block, w_send.at[3 + n], w_recv.at[8 + n], pos=mate)]
        for source, arrival, target in onward:
            if source == n:
                sends.append(remote(block, block, w_send.at[7 + arrival], w_recv.at[arrival], pos=target))
        return sends

    def arrived(n):
        block = shard(n, core)
        return remote(block, block, w_send.at[0], w_recv.at[n], pos=mate)

    def relayed(n):
        block = shard(n, 1 - core)
        return remote(block, block, w_send.at[0], w_recv.at[8 + n], pos=mate)

    for send in own_sends:
        send.start()

    def split_rows(r, block):
        high, low = halves(block.reshape(channels, cols))
        xh[r] = high
        xl[r] = low

    def split_taps(t, carry):
        a, b = t // 3, lax.rem(t, 3)
        high, low = halves(taps[t].T)
        at = pl.ds(pl.multiple_of(b * kept, kept), kept)
        for owner in range(2):
            side = 1 - owner + layer * (2 * owner - 1)
            taken = slice(owner * kept, (owner + 1) * kept)
            wh[a, side, at] = high[taken]
            wl[a, side, at] = low[taken]
        return carry

    lanes = lax.broadcasted_iota(jnp.int32, (kept, cols), 1)

    def swap(k):
        return remote(theirs.at[k], other.at[k], r_send.at[k], r_recv.at[k], layer=1 - layer)

    def convolve(k, sides):
        first_side, count = sides[0], len(sides)
        height = count * 3 * kept
        total = None
        for a in range(3):
            high = jnp.concatenate([xh[2 * k + a], xh[2 * k + a + 1]], axis=1)
            low = jnp.concatenate([xl[2 * k + a], xl[2 * k + a + 1]], axis=1)
            for left, right in ((wh, high), (wl, high), (wh, low)):
                left = left[a, first_side : first_side + count].reshape(height, channels)
                term = jnp.dot(left, right, preferred_element_type=F32)
                total = term if total is None else total + term
        for n, side in enumerate(sides):
            for q in range(2):
                left, middle, right = [
                    total[(3 * n + b) * kept : (3 * n + b + 1) * kept, q * cols : (q + 1) * cols] for b in range(3)
                ]
                left = jnp.where(lanes == 0, 0.0, pltpu.roll(left, 1, 1))
                right = jnp.where(lanes == cols - 1, 0.0, pltpu.roll(right, cols - 1, 1))
                (theirs, ours)[side][k, q] = middle + left + right

    def whole(k, carry):
        convolve(k, (0, 1))
        swap(k).start()
        return carry

    def finish(k, carry):
        swap(k).wait_recv()
        out[pl.ds(2 * k, 2)] = ours[k] + other[k]
        return carry

    def settle(i):
        hop(i, 6, lax.rem(z + 4, RING), up).wait_recv()

    def split_chunk(i):
        for n in range(RUN):
            split_rows(RUN * i + n, ext[:, RUN * i + n])

    def step(t, carry):
        i = t + AHEAD

        @pl.when(i < chunks)
        def _():
            first(i)

        def through(h):
            i = t - (h - 1)

            @pl.when((i >= 0) & (i < chunks))
            def _():
                behind, ahead = lax.rem(z + RING - h, RING), lax.rem(z + h, RING)
                hop(i, 2 * h - 2, behind, up).wait_recv()
                if h < 3:
                    hop(i, 2 * h, behind, up).start()
                hop(i, 2 * h - 1, ahead, down).wait_recv()
                if h < 3:
                    hop(i, 2 * h + 1, ahead, down).start()
                else:
                    source, target = lax.rem(z + RING - 3 * turn, RING), lax.rem(z + RING + turn, RING)

                    @pl.when(i < chunks - 1)
                    def _():
                        hop(i, 6, source, target).start()

                    @pl.when(i == chunks - 1)
                    def _():
                        for n in range(2):
                            part(n, source, target).start()

        fresh = t >= 5
        k = RUN // 2 * (t - 4) - 1

        @pl.when(fresh)
        def _():
            whole(k, 0)

        through(1)

        @pl.when(fresh)
        def _():
            whole(k + 1, 0)

        through(2)

        through(3)

        for early, group in RELAYS:
            @pl.when(t == early)
            def _():
                for d in group:
                    arrived(d).wait_recv()
                    for send in relays(d):
                        send.start()

        @pl.when(t == READY)
        def _():
            local_w.wait()
            remote(filt, weights(mate), w_send.at[0], w_recv.at[0], pos=mate).wait_recv()
            for d in SHARDS:
                relayed(d).wait_recv()
            lax.fori_loop(0, 9, split_taps, 0)

        @pl.when(t == EDGES)
        def _():
            @pl.when(pos > 0)
            def _():
                below.wait_recv()

            @pl.when(pos < places - 1)
            def _():
                above.wait_recv()

            split_rows(0, edge[0])
            split_rows(rows + 1, edge[1])
            whole(0, 0)

        @pl.when(t >= 6)
        def _():
            finish(k - 2, 0)
            finish(k - 1, 0)

        @pl.when(t == 3)
        def _():
            settle(0)

            @pl.when(pos < places - 1)
            def _():
                below.start()

            @pl.when(pos > 0)
            def _():
                above.start()

            split_rows(1, ext[:, 0])
            split_rows(rows, ext[:, 1])
            split_rows(2, ext[:, 2])
            split_rows(3, ext[:, 3])

        @pl.when((t > 3) & (t < chunks + 2))
        def _():
            settle(t - 3)
            split_chunk(t - 3)

        return carry

    lax.fori_loop(0, chunks + 3, step, 0)
    for n in range(2):
        part(n, lax.rem(z + 4, RING), up).wait_recv()
        for at in (rows - 4 + 2 * n, rows - 3 + 2 * n):
            split_rows(at, ext[:, at])
        if n == 0:
            convolve(pairs - 3, (0,))
            swap(pairs - 3).start()
    late = pairs - 2
    lax.fori_loop(late, pairs, lambda k, carry: (convolve(k, (0,)), swap(k).start(), carry)[2], 0)
    lax.fori_loop(late - 1, pairs, lambda k, carry: (convolve(k, (1,)), carry)[1], 0)
    finish(0, 0)
    lax.fori_loop(late - 3, pairs, finish, 0)

    def drain(i, carry):
        for slot in range(6):
            hop(i, slot, z, up).wait_send()

        @pl.when(i < chunks - 1)
        def _():
            hop(i, 6, z, up).wait_send()

        return carry

    lax.fori_loop(0, chunks, drain, 0)

    for n in range(2):
        part(n, z, up).wait_send()

    def drain_swap(k, carry):
        swap(k).wait_send()
        return carry

    lax.fori_loop(0, pairs, drain_swap, 0)
    for send in own_sends:
        send.wait_send()
    for d in SHARDS:
        for send in relays(d):
            send.wait_send()

    @pl.when(pos < places - 1)
    def _():
        below.wait_send()

    @pl.when(pos > 0)
    def _():
        above.wait_send()


def body(activations, filters):
    rows, own, cols = activations.shape
    places = lax.axis_size("pos")
    depth, count = filters.shape[1], filters.shape[2]
    channels = RING * own
    chunks = rows // RUN
    dma = pltpu.SemaphoreType.DMA
    summed = pl.pallas_call(
        kernel,
        out_shape=jax.ShapeDtypeStruct((rows, count // 2, cols), F32),
        in_specs=[pl.BlockSpec(memory_space=pltpu.HBM)] * 2,
        out_specs=pl.BlockSpec(memory_space=pltpu.VMEM),
        scratch_shapes=[
            pltpu.VMEM((RING, rows, own, cols), F32),
            pltpu.VMEM((2, RING, own, cols), F32),
            pltpu.VMEM((9, places * depth, count), F32),
            pltpu.VMEM((rows + 2, channels, cols), BF16),
            pltpu.VMEM((rows + 2, channels, cols), BF16),
            pltpu.VMEM((3, 2, 3 * count // 2, channels), BF16),
            pltpu.VMEM((3, 2, 3 * count // 2, channels), BF16),
            pltpu.VMEM((rows // 2, 2, count // 2, cols), F32),
            pltpu.VMEM((rows // 2, 2, count // 2, cols), F32),
            pltpu.VMEM((rows // 2, 2, count // 2, cols), F32),
            dma((4,)),
            dma((2,)),
            dma((2,)),
            dma((places,)),
            dma((places,)),
            dma((chunks + 1, 7)),
            dma((chunks + 1, 7)),
            dma((rows // 2,)),
            dma((rows // 2,)),
        ],
        compiler_params=pltpu.CompilerParams(
            collective_id=0, has_side_effects=True, vmem_limit_bytes=34 << 20
        ),
    )(pltpu.with_memory_space_constraint(activations, pltpu.HBM), pltpu.with_memory_space_constraint(filters, pltpu.HBM))
    return jnp.maximum(summed, 0.0)


def solution(mesh):
    in_specs = (P("pos", ("layer", "filt"), None), P(None, ("layer", "pos"), "filt"))
    out_specs = P("pos", ("filt", "layer"), None)
    return jax.shard_map(body, mesh=mesh, in_specs=in_specs, out_specs=out_specs, check_vma=False)
```

```python
import jax
import jax.numpy as jnp
from jax import lax
from jax.experimental import pallas as pl
from jax.experimental.pallas import tpu as pltpu
from jax.sharding import PartitionSpec as P

MESH = pl.DeviceIdType.MESH
F32 = jnp.float32
BF16 = jnp.bfloat16
RING = 8
AHEAD = 2
RUN = 4
READY = 3
RELAYS = ((0, (1, 2, 3)), (1, (4, 5, 6)), (2, (7,)))
SHARDS = {1: (0, 1), 2: (-1, 0), 3: (1, 0), 4: (-1, 1), 5: (1, 1), 6: (-2, 0), 7: (2, 1)}
EDGES = 7


def halves(value):
    high = value.astype(BF16)
    return high, (value - high.astype(F32)).astype(BF16)


def kernel(act, filt, out, ext, edge, taps, xh, xl, wh, wl, theirs, ours, other,
           loc_sem, halo_send, halo_recv, w_send, w_recv, z_send, z_recv, r_send, r_recv):
    places = lax.axis_size("pos")
    pos, z, layer = lax.axis_index("pos"), lax.axis_index("filt"), lax.axis_index("layer")
    rows, own, cols = act.shape
    depth = filt.shape[1]
    filters = filt.shape[2]
    channels = RING * own
    chunks = rows // RUN
    pairs = rows // 2
    across = places // 4
    core = lax.rem(pos, 2)
    half = lax.rem(pos // 2, 2)
    facing = pos + 2 - 4 * half
    after, before = lax.rem(pos + 4, places), lax.rem(pos + places - 4, places)
    mate = pos + 1 - 2 * core
    up, down = lax.rem(z + 1, RING), lax.rem(z + RING - 1, RING)
    turn = 1 - 2 * core
    kept = filters // 2

    def remote(src, dst, send, recv, **where):
        return pltpu.make_async_remote_copy(
            src_ref=src, dst_ref=dst, send_sem=send, recv_sem=recv,
            device_id=where, device_id_type=MESH,
        )

    def panel(source, i):
        return ext.at[source, pl.ds(RUN * i, RUN)]

    def hop(i, slot, source, target):
        block = panel(source, i)
        return remote(block, block, z_send.at[i, slot], z_recv.at[i, slot], filt=target)

    def weights(place):
        return taps.at[:, pl.ds(pl.multiple_of(place * depth, depth), depth)]

    local = [
        pltpu.make_async_copy(act.at[0], ext.at[z, 0], loc_sem.at[0]),
        pltpu.make_async_copy(act.at[rows - 1], ext.at[z, 1], loc_sem.at[2]),
        pltpu.make_async_copy(act.at[pl.ds(1, rows - 2)], ext.at[z, pl.ds(2, rows - 2)], loc_sem.at[3]),
    ]
    for copy in local:
        copy.start()
    local_w = pltpu.make_async_copy(filt, weights(pos), loc_sem.at[1])
    local_w.start()

    @pl.when(pos == 0)
    def _():
        edge[0] = jnp.zeros((RING, own, cols), F32)

    @pl.when(pos == places - 1)
    def _():
        edge[1] = jnp.zeros((RING, own, cols), F32)

    barrier = pltpu.get_barrier_semaphore()
    pl.semaphore_signal(barrier, inc=1, device_id={"filt": up}, device_id_type=MESH)
    pl.semaphore_signal(barrier, inc=1, device_id={"filt": down}, device_id_type=MESH)
    pl.semaphore_signal(barrier, inc=1, device_id={"layer": 1 - layer}, device_id_type=MESH)
    near = (lax.rem(pos + 1, places), lax.rem(pos + places - 1, places), after, before, facing)
    for place in near:
        pl.semaphore_signal(barrier, inc=1, device_id={"pos": place}, device_id_type=MESH)
    pl.semaphore_wait(barrier, len(near) + 3)

    below = remote(ext.at[:, 1], edge.at[0], halo_send.at[0], halo_recv.at[0], pos=lax.rem(pos + 1, places))
    above = remote(ext.at[:, 0], edge.at[1], halo_send.at[1], halo_recv.at[1], pos=lax.rem(pos + places - 1, places))

    def part(n, source, target):
        block = ext.at[source, pl.ds(RUN * (chunks - 1) + 2 * n, 2)]
        at = chunks - 1 + n
        return remote(block, block, z_send.at[at, 6], z_recv.at[at, 6], filt=target)

    def first(i):
        hop(i, core, z, lax.rem(z + RING + turn, RING)).start()
        hop(i, 1 - core, z, lax.rem(z + RING - turn, RING)).start()

    for copy in local:
        copy.wait()
    for i in range(AHEAD):
        first(i)
    def shard(n, side):
        dx, flip = SHARDS[n]
        row = lax.rem(pos // 4 + across + dx, across)
        return weights(4 * row + 2 * (1 - half if flip else half) + side)

    own_sends = [
        remote(filt, weights(pos), w_send.at[0], w_recv.at[0], pos=mate),
        remote(filt, weights(pos), w_send.at[1], w_recv.at[1], pos=facing),
        remote(filt, weights(pos), w_send.at[2], w_recv.at[2], pos=after),
        remote(filt, weights(pos), w_send.at[3], w_recv.at[3], pos=before),
    ]
    onward = ((1, 4, after), (1, 5, before), (2, 6, after), (5, 7, before))

    def relays(n):
        block = shard(n, core)
        sends = [remote(block, block, w_send.at[3 + n], w_recv.at[8 + n], pos=mate)]
        for source, arrival, target in onward:
            if source == n:
                sends.append(remote(block, block, w_send.at[7 + arrival], w_recv.at[arrival], pos=target))
        return sends

    def arrived(n):
        block = shard(n, core)
        return remote(block, block, w_send.at[0], w_recv.at[n], pos=mate)

    def relayed(n):
        block = shard(n, 1 - core)
        return remote(block, block, w_send.at[0], w_recv.at[8 + n], pos=mate)

    for send in own_sends:
        send.start()

    def split_rows(r, block):
        high, low = halves(block.reshape(channels, cols))
        xh[r] = high
        xl[r] = low

    def split_taps(t, carry):
        a, b = t // 3, lax.rem(t, 3)
        high, low = halves(taps[t].T)
        at = pl.ds(pl.multiple_of(b * kept, kept), kept)
        for owner in range(2):
            side = 1 - owner + layer * (2 * owner - 1)
            taken = slice(owner * kept, (owner + 1) * kept)
            wh[a, side, at] = high[taken]
            wl[a, side, at] = low[taken]
        return carry

    lanes = lax.broadcasted_iota(jnp.int32, (kept, cols), 1)

    def swap(k):
        return remote(theirs.at[k], other.at[k], r_send.at[k], r_recv.at[k], layer=1 - layer)

    def convolve(k, sides):
        first_side, count = sides[0], len(sides)
        height = count * 3 * kept
        total = None
        for a in range(3):
            high = jnp.concatenate([xh[2 * k + a], xh[2 * k + a + 1]], axis=1)
            low = jnp.concatenate([xl[2 * k + a], xl[2 * k + a + 1]], axis=1)
            for left, right in ((wh, high), (wl, high), (wh, low)):
                left = left[a, first_side : first_side + count].reshape(height, channels)
                term = jnp.dot(left, right, preferred_element_type=F32)
                total = term if total is None else total + term
        for n, side in enumerate(sides):
            for q in range(2):
                left, middle, right = [
                    total[(3 * n + b) * kept : (3 * n + b + 1) * kept, q * cols : (q + 1) * cols] for b in range(3)
                ]
                left = jnp.where(lanes == 0, 0.0, pltpu.roll(left, 1, 1))
                right = jnp.where(lanes == cols - 1, 0.0, pltpu.roll(right, cols - 1, 1))
                (theirs, ours)[side][k, q] = middle + left + right

    def whole(k, carry):
        convolve(k, (0, 1))
        swap(k).start()
        return carry

    def finish(k, carry):
        swap(k).wait_recv()
        out[pl.ds(2 * k, 2)] = ours[k] + other[k]
        return carry

    def settle(i):
        hop(i, 6, lax.rem(z + 4, RING), up).wait_recv()

    def split_chunk(i):
        for n in range(RUN):
            split_rows(RUN * i + n, ext[:, RUN * i + n])

    def step(t, carry):
        i = t + AHEAD

        @pl.when(i < chunks)
        def _():
            first(i)

        def through(h):
            i = t - (h - 1)

            @pl.when((i >= 0) & (i < chunks))
            def _():
                hop(i, 2 * h - 2 + core, lax.rem(z + RING - h * turn, RING), up).wait_recv()
                if h < 3:
                    hop(i, 2 * h + core, lax.rem(z + RING - h * turn, RING), lax.rem(z + RING + turn, RING)).start()
                    hop(i, 2 * h - 1 - core, lax.rem(z + RING + h * turn, RING), up).wait_recv()
                    hop(i, 2 * h + 1 - core, lax.rem(z + RING + h * turn, RING), lax.rem(z + RING - turn, RING)).start()
                else:
                    source, target = lax.rem(z + RING - 3 * turn, RING), lax.rem(z + RING + turn, RING)

                    @pl.when(i < chunks - 1)
                    def _():
                        hop(i, 6, source, target).start()

                    @pl.when(i == chunks - 1)
                    def _():
                        for n in range(2):
                            part(n, source, target).start()

                    hop(i, 2 * h - 1 - core, lax.rem(z + RING + h * turn, RING), up).wait_recv()

        fresh = t >= 5
        k = RUN // 2 * (t - 4) - 1

        @pl.when(t == EDGES)
        def _():
            @pl.when(pos > 0)
            def _():
                below.wait_recv()

            @pl.when(pos < places - 1)
            def _():
                above.wait_recv()

            split_rows(0, edge[0])
            split_rows(rows + 1, edge[1])
            whole(0, 0)

        @pl.when(fresh)
        def _():
            whole(k, 0)

        through(1)

        @pl.when(fresh)
        def _():
            whole(k + 1, 0)

        through(2)

        through(3)

        for early, group in RELAYS:
            @pl.when(t == early)
            def _():
                for d in group:
                    arrived(d).wait_recv()
                    for send in relays(d):
                        send.start()

        @pl.when(t == READY)
        def _():
            local_w.wait()
            remote(filt, weights(mate), w_send.at[0], w_recv.at[0], pos=mate).wait_recv()
            for d in SHARDS:
                relayed(d).wait_recv()
            lax.fori_loop(0, 9, split_taps, 0)

        @pl.when(t == 3)
        def _():
            settle(0)

            @pl.when(pos < places - 1)
            def _():
                below.start()

            @pl.when(pos > 0)
            def _():
                above.start()

            split_rows(1, ext[:, 0])
            split_rows(rows, ext[:, 1])
            split_rows(2, ext[:, 2])
            split_rows(3, ext[:, 3])

        @pl.when((t > 3) & (t < chunks + 2))
        def _():
            settle(t - 3)
            split_chunk(t - 3)

        @pl.when(t >= 6)
        def _():
            finish(k - 2, 0)
            finish(k - 1, 0)

        return carry

    lax.fori_loop(0, chunks + 3, step, 0)
    for n in range(2):
        part(n, lax.rem(z + 4, RING), up).wait_recv()
        for at in (rows - 4 + 2 * n, rows - 3 + 2 * n):
            split_rows(at, ext[:, at])
        if n == 0:
            convolve(pairs - 3, (0,))
            swap(pairs - 3).start()
    late = pairs - 2
    lax.fori_loop(late, pairs, lambda k, carry: (convolve(k, (0,)), swap(k).start(), carry)[2], 0)
    lax.fori_loop(late - 1, pairs, lambda k, carry: (convolve(k, (1,)), carry)[1], 0)
    finish(0, 0)
    lax.fori_loop(late - 3, pairs, finish, 0)

    def drain(i, carry):
        for slot in range(6):
            hop(i, slot, z, up).wait_send()

        @pl.when(i < chunks - 1)
        def _():
            hop(i, 6, z, up).wait_send()

        return carry

    lax.fori_loop(0, chunks, drain, 0)

    for n in range(2):
        part(n, z, up).wait_send()

    def drain_swap(k, carry):
        swap(k).wait_send()
        return carry

    lax.fori_loop(0, pairs, drain_swap, 0)
    for send in own_sends:
        send.wait_send()
    for d in SHARDS:
        for send in relays(d):
            send.wait_send()

    @pl.when(pos < places - 1)
    def _():
        below.wait_send()

    @pl.when(pos > 0)
    def _():
        above.wait_send()


def body(activations, filters):
    rows, own, cols = activations.shape
    places = lax.axis_size("pos")
    depth, count = filters.shape[1], filters.shape[2]
    channels = RING * own
    chunks = rows // RUN
    dma = pltpu.SemaphoreType.DMA
    summed = pl.pallas_call(
        kernel,
        out_shape=jax.ShapeDtypeStruct((rows, count // 2, cols), F32),
        in_specs=[pl.BlockSpec(memory_space=pltpu.HBM)] * 2,
        out_specs=pl.BlockSpec(memory_space=pltpu.VMEM),
        scratch_shapes=[
            pltpu.VMEM((RING, rows, own, cols), F32),
            pltpu.VMEM((2, RING, own, cols), F32),
            pltpu.VMEM((9, places * depth, count), F32),
            pltpu.VMEM((rows + 2, channels, cols), BF16),
            pltpu.VMEM((rows + 2, channels, cols), BF16),
            pltpu.VMEM((3, 2, 3 * count // 2, channels), BF16),
            pltpu.VMEM((3, 2, 3 * count // 2, channels), BF16),
            pltpu.VMEM((rows // 2, 2, count // 2, cols), F32),
            pltpu.VMEM((rows // 2, 2, count // 2, cols), F32),
            pltpu.VMEM((rows // 2, 2, count // 2, cols), F32),
            dma((4,)),
            dma((2,)),
            dma((2,)),
            dma((places,)),
            dma((places,)),
            dma((chunks + 1, 7)),
            dma((chunks + 1, 7)),
            dma((rows // 2,)),
            dma((rows // 2,)),
        ],
        compiler_params=pltpu.CompilerParams(
            collective_id=0, has_side_effects=True, vmem_limit_bytes=34 << 20
        ),
    )(pltpu.with_memory_space_constraint(activations, pltpu.HBM), pltpu.with_memory_space_constraint(filters, pltpu.HBM))
    return jnp.maximum(summed, 0.0)


def solution(mesh):
    in_specs = (P("pos", ("layer", "filt"), None), P(None, ("layer", "pos"), "filt"))
    out_specs = P("pos", ("filt", "layer"), None)
    return jax.shard_map(body, mesh=mesh, in_specs=in_specs, out_specs=out_specs, check_vma=False)
```

```python
import jax
import jax.numpy as jnp
from jax import lax
from jax.experimental import pallas as pl
from jax.experimental.pallas import tpu as pltpu
from jax.sharding import PartitionSpec as P

MESH = pl.DeviceIdType.MESH
F32 = jnp.float32
BF16 = jnp.bfloat16
RING = 8
AHEAD = 2
RUN = 4
READY = 3
RELAYS = ((0, (1, 2, 3)), (1, (4, 5, 6)), (2, (7,)))
SHARDS = {1: (0, 1), 2: (-1, 0), 3: (1, 0), 4: (-1, 1), 5: (1, 1), 6: (-2, 0), 7: (2, 1)}
EDGES = 7


def halves(value):
    high = value.astype(BF16)
    return high, (value - high.astype(F32)).astype(BF16)


def kernel(act, filt, out, ext, edge, taps, xh, xl, wh, wl, theirs, ours, other,
           loc_sem, halo_send, halo_recv, w_send, w_recv, z_send, z_recv, r_send, r_recv):
    places = lax.axis_size("pos")
    pos, z, layer = lax.axis_index("pos"), lax.axis_index("filt"), lax.axis_index("layer")
    rows, own, cols = act.shape
    depth = filt.shape[1]
    filters = filt.shape[2]
    channels = RING * own
    chunks = rows // RUN
    pairs = rows // 2
    across = places // 4
    core = lax.rem(pos, 2)
    half = lax.rem(pos // 2, 2)
    facing = pos + 2 - 4 * half
    after, before = lax.rem(pos + 4, places), lax.rem(pos + places - 4, places)
    mate = pos + 1 - 2 * core
    up, down = lax.rem(z + 1, RING), lax.rem(z + RING - 1, RING)
    turn = 1 - 2 * core
    kept = filters // 2

    def remote(src, dst, send, recv, **where):
        return pltpu.make_async_remote_copy(
            src_ref=src, dst_ref=dst, send_sem=send, recv_sem=recv,
            device_id=where, device_id_type=MESH,
        )

    def panel(source, i):
        return ext.at[source, pl.ds(RUN * i, RUN)]

    def hop(i, slot, source, target):
        block = panel(source, i)
        return remote(block, block, z_send.at[i, slot], z_recv.at[i, slot], filt=target)

    def weights(place):
        return taps.at[:, pl.ds(pl.multiple_of(place * depth, depth), depth)]

    local = [
        pltpu.make_async_copy(act.at[0], ext.at[z, 0], loc_sem.at[0]),
        pltpu.make_async_copy(act.at[rows - 1], ext.at[z, 1], loc_sem.at[2]),
        pltpu.make_async_copy(act.at[pl.ds(1, rows - 2)], ext.at[z, pl.ds(2, rows - 2)], loc_sem.at[3]),
    ]
    for copy in local:
        copy.start()
    local_w = pltpu.make_async_copy(filt, weights(pos), loc_sem.at[1])
    local_w.start()

    @pl.when(pos == 0)
    def _():
        edge[0] = jnp.zeros((RING, own, cols), F32)

    @pl.when(pos == places - 1)
    def _():
        edge[1] = jnp.zeros((RING, own, cols), F32)

    barrier = pltpu.get_barrier_semaphore()
    pl.semaphore_signal(barrier, inc=1, device_id={"filt": up}, device_id_type=MESH)
    pl.semaphore_signal(barrier, inc=1, device_id={"filt": down}, device_id_type=MESH)
    pl.semaphore_signal(barrier, inc=1, device_id={"layer": 1 - layer}, device_id_type=MESH)
    near = (lax.rem(pos + 1, places), lax.rem(pos + places - 1, places), after, before, facing)
    for place in near:
        pl.semaphore_signal(barrier, inc=1, device_id={"pos": place}, device_id_type=MESH)
    pl.semaphore_wait(barrier, len(near) + 3)

    below = remote(ext.at[:, 1], edge.at[0], halo_send.at[0], halo_recv.at[0], pos=lax.rem(pos + 1, places))
    above = remote(ext.at[:, 0], edge.at[1], halo_send.at[1], halo_recv.at[1], pos=lax.rem(pos + places - 1, places))

    def part(n, source, target):
        block = ext.at[source, pl.ds(RUN * (chunks - 1) + 2 * n, 2)]
        at = chunks - 1 + n
        return remote(block, block, z_send.at[at, 6], z_recv.at[at, 6], filt=target)

    def first(i):
        hop(i, 0, z, up).start()
        hop(i, 1, z, down).start()

    for copy in local:
        copy.wait()
    for i in range(AHEAD):
        first(i)
    def shard(n, side):
        dx, flip = SHARDS[n]
        row = lax.rem(pos // 4 + across + dx, across)
        return weights(4 * row + 2 * (1 - half if flip else half) + side)

    own_sends = [
        remote(filt, weights(pos), w_send.at[0], w_recv.at[0], pos=mate),
        remote(filt, weights(pos), w_send.at[1], w_recv.at[1], pos=facing),
        remote(filt, weights(pos), w_send.at[2], w_recv.at[2], pos=after),
        remote(filt, weights(pos), w_send.at[3], w_recv.at[3], pos=before),
    ]
    onward = ((1, 4, after), (1, 5, before), (2, 6, after), (5, 7, before))

    def relays(n):
        block = shard(n, core)
        sends = [remote(block, block, w_send.at[3 + n], w_recv.at[8 + n], pos=mate)]
        for source, arrival, target in onward:
            if source == n:
                sends.append(remote(block, block, w_send.at[7 + arrival], w_recv.at[arrival], pos=target))
        return sends

    def arrived(n):
        block = shard(n, core)
        return remote(block, block, w_send.at[0], w_recv.at[n], pos=mate)

    def relayed(n):
        block = shard(n, 1 - core)
        return remote(block, block, w_send.at[0], w_recv.at[8 + n], pos=mate)

    for send in own_sends:
        send.start()

    def split_rows(r, block):
        high, low = halves(block.reshape(channels, cols))
        xh[r] = high
        xl[r] = low

    def split_taps(t, carry):
        a, b = t // 3, lax.rem(t, 3)
        high, low = halves(taps[t].T)
        at = pl.ds(pl.multiple_of(b * kept, kept), kept)
        for owner in range(2):
            side = 1 - owner + layer * (2 * owner - 1)
            taken = slice(owner * kept, (owner + 1) * kept)
            wh[a, side, at] = high[taken]
            wl[a, side, at] = low[taken]
        return carry

    lanes = lax.broadcasted_iota(jnp.int32, (kept, cols), 1)

    def swap(k):
        return remote(theirs.at[k], other.at[k], r_send.at[k], r_recv.at[k], layer=1 - layer)

    def convolve(k, sides):
        first_side, count = sides[0], len(sides)
        height = count * 3 * kept
        total = None
        for a in range(3):
            high = jnp.concatenate([xh[2 * k + a], xh[2 * k + a + 1]], axis=1)
            low = jnp.concatenate([xl[2 * k + a], xl[2 * k + a + 1]], axis=1)
            for left, right in ((wh, high), (wl, high), (wh, low)):
                left = left[a, first_side : first_side + count].reshape(height, channels)
                term = jnp.dot(left, right, preferred_element_type=F32)
                total = term if total is None else total + term
        for n, side in enumerate(sides):
            for q in range(2):
                left, middle, right = [
                    total[(3 * n + b) * kept : (3 * n + b + 1) * kept, q * cols : (q + 1) * cols] for b in range(3)
                ]
                left = jnp.where(lanes == 0, 0.0, pltpu.roll(left, 1, 1))
                right = jnp.where(lanes == cols - 1, 0.0, pltpu.roll(right, cols - 1, 1))
                (theirs, ours)[side][k, q] = middle + left + right

    def whole(k, carry):
        convolve(k, (0, 1))
        swap(k).start()
        return carry

    def finish(k, carry):
        swap(k).wait_recv()
        out[pl.ds(2 * k, 2)] = ours[k] + other[k]
        return carry

    def settle(i):
        hop(i, 6, lax.rem(z + 4, RING), up).wait_recv()

    def split_chunk(i):
        for n in range(RUN):
            split_rows(RUN * i + n, ext[:, RUN * i + n])

    def step(t, carry):
        i = t + AHEAD

        @pl.when(i < chunks)
        def _():
            first(i)

        def through(h):
            i = t - (h - 1)

            @pl.when((i >= 0) & (i < chunks))
            def _():
                behind, ahead = lax.rem(z + RING - h, RING), lax.rem(z + h, RING)
                hop(i, 2 * h - 2, behind, up).wait_recv()
                if h < 3:
                    hop(i, 2 * h, behind, up).start()
                hop(i, 2 * h - 1, ahead, down).wait_recv()
                if h < 3:
                    hop(i, 2 * h + 1, ahead, down).start()
                else:
                    source, target = lax.rem(z + RING - 3 * turn, RING), lax.rem(z + RING + turn, RING)

                    @pl.when(i < chunks - 1)
                    def _():
                        hop(i, 6, source, target).start()

                    @pl.when(i == chunks - 1)
                    def _():
                        for n in range(2):
                            part(n, source, target).start()

        fresh = t >= 5
        k = RUN // 2 * (t - 4) - 1

        @pl.when(t == EDGES)
        def _():
            @pl.when(pos > 0)
            def _():
                below.wait_recv()

            @pl.when(pos < places - 1)
            def _():
                above.wait_recv()

            split_rows(0, edge[0])
            split_rows(rows + 1, edge[1])
            whole(0, 0)

        @pl.when(fresh)
        def _():
            whole(k, 0)

        through(1)

        @pl.when(fresh)
        def _():
            whole(k + 1, 0)

        through(2)

        through(3)

        for early, group in RELAYS:
            @pl.when(t == early)
            def _():
                for d in group:
                    arrived(d).wait_recv()
                    for send in relays(d):
                        send.start()

        @pl.when(t == READY)
        def _():
            local_w.wait()
            remote(filt, weights(mate), w_send.at[0], w_recv.at[0], pos=mate).wait_recv()
            for d in SHARDS:
                relayed(d).wait_recv()
            lax.fori_loop(0, 9, split_taps, 0)

        @pl.when(t >= 6)
        def _():
            finish(k - 2, 0)
            finish(k - 1, 0)

        @pl.when(t == 3)
        def _():
            settle(0)

            @pl.when(pos < places - 1)
            def _():
                below.start()

            @pl.when(pos > 0)
            def _():
                above.start()

            split_rows(1, ext[:, 0])
            split_rows(rows, ext[:, 1])
            split_rows(2, ext[:, 2])
            split_rows(3, ext[:, 3])

        @pl.when((t > 3) & (t < chunks + 2))
        def _():
            settle(t - 3)
            split_chunk(t - 3)

        return carry

    lax.fori_loop(0, chunks + 3, step, 0)
    for n in range(2):
        part(n, lax.rem(z + 4, RING), up).wait_recv()
        for at in (rows - 4 + 2 * n, rows - 3 + 2 * n):
            split_rows(at, ext[:, at])
        if n == 0:
            convolve(pairs - 3, (0,))
            swap(pairs - 3).start()
    late = pairs - 2
    lax.fori_loop(late, pairs, lambda k, carry: (convolve(k, (0,)), swap(k).start(), carry)[2], 0)
    lax.fori_loop(late - 1, pairs, lambda k, carry: (convolve(k, (1,)), carry)[1], 0)
    finish(0, 0)
    lax.fori_loop(late - 3, pairs, finish, 0)

    def drain(i, carry):
        for slot in range(6):
            hop(i, slot, z, up).wait_send()

        @pl.when(i < chunks - 1)
        def _():
            hop(i, 6, z, up).wait_send()

        return carry

    lax.fori_loop(0, chunks, drain, 0)

    for n in range(2):
        part(n, z, up).wait_send()

    def drain_swap(k, carry):
        swap(k).wait_send()
        return carry

    lax.fori_loop(0, pairs, drain_swap, 0)
    for send in own_sends:
        send.wait_send()
    for d in SHARDS:
        for send in relays(d):
            send.wait_send()

    @pl.when(pos < places - 1)
    def _():
        below.wait_send()

    @pl.when(pos > 0)
    def _():
        above.wait_send()


def body(activations, filters):
    rows, own, cols = activations.shape
    places = lax.axis_size("pos")
    depth, count = filters.shape[1], filters.shape[2]
    channels = RING * own
    chunks = rows // RUN
    dma = pltpu.SemaphoreType.DMA
    summed = pl.pallas_call(
        kernel,
        out_shape=jax.ShapeDtypeStruct((rows, count // 2, cols), F32),
        in_specs=[pl.BlockSpec(memory_space=pltpu.HBM)] * 2,
        out_specs=pl.BlockSpec(memory_space=pltpu.VMEM),
        scratch_shapes=[
            pltpu.VMEM((RING, rows, own, cols), F32),
            pltpu.VMEM((2, RING, own, cols), F32),
            pltpu.VMEM((9, places * depth, count), F32),
            pltpu.VMEM((rows + 2, channels, cols), BF16),
            pltpu.VMEM((rows + 2, channels, cols), BF16),
            pltpu.VMEM((3, 2, 3 * count // 2, channels), BF16),
            pltpu.VMEM((3, 2, 3 * count // 2, channels), BF16),
            pltpu.VMEM((rows // 2, 2, count // 2, cols), F32),
            pltpu.VMEM((rows // 2, 2, count // 2, cols), F32),
            pltpu.VMEM((rows // 2, 2, count // 2, cols), F32),
            dma((4,)),
            dma((2,)),
            dma((2,)),
            dma((places,)),
            dma((places,)),
            dma((chunks + 1, 7)),
            dma((chunks + 1, 7)),
            dma((rows // 2,)),
            dma((rows // 2,)),
        ],
        compiler_params=pltpu.CompilerParams(
            collective_id=0, has_side_effects=True, vmem_limit_bytes=34 << 20
        ),
    )(pltpu.with_memory_space_constraint(activations, pltpu.HBM), pltpu.with_memory_space_constraint(filters, pltpu.HBM))
    return jnp.maximum(summed, 0.0)


def solution(mesh):
    in_specs = (P("pos", ("layer", "filt"), None), P(None, ("layer", "pos"), "filt"))
    out_specs = P("pos", ("filt", "layer"), None)
    return jax.shard_map(body, mesh=mesh, in_specs=in_specs, out_specs=out_specs, check_vma=False)
```
